256 devices in a mesh: prow: 16 (over z, core), pcol: 16 (over y, x).
Axes of the slice: x: 4, y: 4, z: 8, core: 2. Of those that a mesh axis runs over, the one named last changes fastest.
Arguments:
- diag_tile: float32 [512, 512], P('prow', 'pcol'), as said below
- panel: float32 [2, 16, 512, 512], P(None, 'prow', None, 'pcol'), may hold values from -0.3 to 0.3
- trailing: float32 [2, 16, 512, 2, 16, 512], P(None, 'prow', None, None, 'pcol'), may hold values from -6 to 6
- kept: int32 [33, 33], replicated, may hold values from 0 to 1, as said below
- precision: int32 [33, 33], replicated, may hold values from 0 to 1, as said below
- tile_scale: float32 [33, 33], replicated, may hold values from 0.5 to 4
Outputs:
- diag_factor: float32 [512, 512], P('prow', 'pcol')
- factor: float32 [2, 16, 512, 512], P(None, 'prow', None, 'pcol')
- updated: float32 [2, 16, 512, 2, 16, 512], P(None, 'prow', None, None, 'pcol')
The draws below stay inside these ranges and needn't reach their ends.
Inputs may be any that keep to these rules, and one draw needn't show every extreme that they name: kept is symmetric, 1 on the diagonal, and has zeros in every draw; tiles are kept by a distance between the tiles' places. precision is symmetric, 1 on the diagonal, has zeros in every draw, and is 1 only where kept is 1. diag_tile is symmetric positive definite with smallest eigenvalue at least 0.1.
All inputs are finite; a program needn't handle non-finite values.
Results may differ from the reference program's by a relative error of at most 0.0003.
The reference program's roundings to bfloat16 on the way count: a program that leaves them out, or rounds other values in their place, can miss the bound.
Values sent between devices are 32-bit elements; how exact they have to be, the bound alone decides.
A program may use at most 64 MiB of HBM per device.

```python
import math
import jax
import jax.numpy as jnp
from jax import lax

NB = 512
ROW_TILES = 2
TILES = 32
COL_TILES = 2
N_PROW = 16
N_PCOL = 16


def tile_layout(key):
    places = jax.random.randint(jax.random.fold_in(key, 11), (TILES + 1, 2), 0, 6)
    places = places.at[1].set(jnp.array([0, 0], dtype=places.dtype))
    places = places.at[TILES].set(jnp.array([5, 5], dtype=places.dtype))
    spread = jnp.abs(places[:, None, :] - places[None, :, :])
    reach = spread[:, :, 0] + spread[:, :, 1]
    return ((reach <= 4).astype(jnp.int32), (reach <= 1).astype(jnp.int32))


def draw_kept(key, part):
    return tile_layout(key)[0]


def draw_precision(key, part):
    return tile_layout(key)[1]


def draw_diag_tile(key, part):
    index = jnp.arange(NB, dtype=jnp.int32)
    across = (index % 16).astype(jnp.float32)
    down = (index // 16).astype(jnp.float32)
    jitter = jax.random.uniform(jax.random.fold_in(key, 3), (2, NB), jnp.float32, -0.3, 0.3)
    place_x = across + jitter[0]
    place_y = down + jitter[1]
    delta_x = place_x[:, None] - place_x[None, :]
    delta_y = place_y[:, None] - place_y[None, :]
    distance = jnp.sqrt(delta_x * delta_x + delta_y * delta_y)
    length = 2.0
    identity = jnp.eye(NB, dtype=jnp.float32)
    return jnp.exp(distance * (-1.0 / length)) + 0.1 * identity


def block_levels(key, extent, split, smallest, largest):
    level, own = 1.0, jax.random.fold_in(key, 6)
    for position, blocks in split:
        steps = jnp.exp(jax.random.uniform(jax.random.fold_in(own, position), (blocks,), jnp.float32, smallest / len(split), largest / len(split)))
        level = level * jnp.repeat(steps, extent[position] // blocks).reshape([-1 if axis == position else 1 for axis in range(len(extent))])
    return level


def gaussian(key, extent, scale, limit, split=(), kind=jnp.bfloat16):
    drawn = jax.random.normal(key, extent, jnp.float32) * scale
    if len(split) > 0:
        drawn = block_levels(key, extent, split, -0.22, 0.18) * drawn
    return jnp.clip(drawn, min=-limit, max=limit).astype(kind)


def setup_inputs(seed: int = 0) -> dict:
    arg_keys = jax.random.split(jax.random.key(seed), 7)
    return {
        "diag_tile": draw_diag_tile(jax.random.fold_in(arg_keys[6], 71), 0),
        "panel": gaussian(arg_keys[1], (ROW_TILES, N_PROW, NB, NB), 0.05, 0.3, ((1, 16), (3, 16)), jnp.float32),
        "trailing": gaussian(arg_keys[2], (ROW_TILES, N_PROW, NB, COL_TILES, N_PCOL, NB), 1.0, 6.0, ((1, 16), (4, 16)), jnp.float32),
        "kept": draw_kept(jax.random.fold_in(arg_keys[6], 71), 0),
        "precision": draw_precision(jax.random.fold_in(arg_keys[6], 71), 0),
        "tile_scale": jnp.clip(jnp.exp(jax.random.uniform(arg_keys[5], (TILES + 1, TILES + 1), jnp.float32, math.log(0.5), math.log(4.0))), 0.5, 4.0),
    }


def solve_panel(factor_lower, panel_rows):
    return jax.scipy.linalg.solve_triangular(factor_lower, panel_rows.T, lower=True).T

def reference(diag_tile, panel, trailing, kept, precision, tile_scale):
    tiles_all = ROW_TILES * N_PROW
    diag_factor = jnp.linalg.cholesky(diag_tile)
    solved = solve_panel(diag_factor, panel.reshape(tiles_all * NB, NB))
    panel_keep = kept[1:, 0].astype(jnp.float32)
    factor = solved.reshape(tiles_all, NB, NB) * panel_keep[:, None, None]
    factor_flat = factor.reshape(tiles_all * NB, NB)
    factor_half = factor_flat.astype(jnp.bfloat16)
    matrix = trailing.reshape(tiles_all * NB, tiles_all * NB)

    def one_row(index):
        start = index * NB
        row_block = lax.dynamic_slice_in_dim(matrix, start, NB, 0)
        row_factor = lax.dynamic_slice_in_dim(factor_flat, start, NB, 0)
        row_half = lax.dynamic_slice_in_dim(factor_half, start, NB, 0)
        exact = jnp.dot(row_factor.astype(jnp.float32), factor_flat.T.astype(jnp.float32), precision=lax.Precision.HIGHEST, preferred_element_type=jnp.float32)
        rough = jnp.dot(row_half.astype(jnp.float32), factor_half.T.astype(jnp.float32), preferred_element_type=jnp.float32)
        keep_row = jnp.repeat(lax.dynamic_index_in_dim(kept, index + 1, 0, keepdims=False)[1:], NB)
        near_row = jnp.repeat(lax.dynamic_index_in_dim(precision, index + 1, 0, keepdims=False)[1:], NB)
        scale_row = jnp.repeat(lax.dynamic_index_in_dim(tile_scale, index + 1, 0, keepdims=False)[1:], NB)
        near_value = row_block - exact
        far_half = (row_block - rough / scale_row[None, :]).astype(jnp.bfloat16)
        far_value = lax.optimization_barrier(far_half).astype(jnp.float32)
        return jnp.where(keep_row[None, :] == 1, jnp.where(near_row[None, :] == 1, near_value, far_value), jnp.float32(0.0))
    updated = lax.map(one_row, jnp.arange(tiles_all, dtype=jnp.int32))
    return (diag_factor, factor.reshape(panel.shape), updated.reshape(trailing.shape))
```

```python
import jax
import jax.numpy as jnp
from jax import lax
from jax.sharding import PartitionSpec as P


def per_device(diag_tile, panel, trailing, kept, precision, tile_scale):
    row_devices = lax.axis_size("prow")
    col_devices = lax.axis_size("pcol")
    row_index = lax.axis_index("prow")
    col_index = lax.axis_index("pcol")
    row_tiles = panel.shape[0]
    tile_width = panel.shape[2]
    col_tiles = row_tiles * row_devices // col_devices
    piece_rows = tile_width // row_devices
    piece_cols = tile_width // col_devices
    own = jnp.transpose(panel[:, 0], (0, 2, 1))
    flip = [
        (a * col_devices + b, b * col_devices + a)
        for a in range(row_devices)
        for b in range(col_devices)
    ]
    turned = lax.ppermute(own, ("prow", "pcol"), flip)
    diag_piece = lax.all_gather(diag_tile, "pcol", axis=1, tiled=True)
    diag_whole = lax.all_gather(diag_piece, "prow", axis=0, tiled=True)
    rows_t = lax.all_gather(own, "pcol", axis=0)
    cols_t = lax.all_gather(turned, "prow", axis=0)
    diag_lower = jnp.linalg.cholesky(diag_whole)
    diag_out = lax.dynamic_slice(
        diag_lower, (row_index * piece_rows, col_index * piece_cols), (piece_rows, piece_cols)
    )
    both = jnp.stack([rows_t, cols_t], 2)
    both = both.transpose(0, 3, 2, 1, 4).reshape(tile_width, 2 * row_tiles * tile_width)
    solved = jax.scipy.linalg.solve_triangular(diag_lower, both, lower=True)
    solved = solved.reshape(tile_width, 2, row_tiles, tile_width)
    grid_keep = kept[1:, 0].reshape(row_tiles, row_devices)
    row_keep = lax.dynamic_index_in_dim(grid_keep, row_index, 1, keepdims=False)
    col_keep = lax.dynamic_index_in_dim(grid_keep, col_index, 1, keepdims=False)
    keep = jnp.stack([row_keep, col_keep], 0).astype(jnp.float32)
    factors = solved * keep[None, :, :, None]
    row_factor, col_factor = factors[:, 0], factors[:, 1]
    factor_out = lax.dynamic_slice_in_dim(row_factor, col_index * piece_cols, piece_cols, 0)
    factor_out = factor_out.transpose(1, 2, 0)[:, None]

    def own_tiles(table):
        grid = table[1:, 1:].reshape(row_tiles, row_devices, col_tiles, col_devices)
        return lax.dynamic_index_in_dim(
            lax.dynamic_index_in_dim(grid, row_index, 1, False), col_index, 2, False
        )

    keep_tiles = own_tiles(kept)
    near_tiles = own_tiles(precision)
    scale_tiles = own_tiles(tile_scale)
    current = trailing.reshape(row_tiles, tile_width, col_tiles, tile_width)
    row_half = row_factor.astype(jnp.bfloat16)
    col_half = col_factor.astype(jnp.bfloat16)
    exact = jnp.einsum(
        "nra,ntb->ratb",
        row_factor,
        col_factor,
        precision=lax.Precision.HIGHEST,
        preferred_element_type=jnp.float32,
    )
    rough = jnp.einsum("nra,ntb->ratb", row_half, col_half, preferred_element_type=jnp.float32)
    near_value = current - exact
    far_half = (current - rough / scale_tiles[:, None, :, None]).astype(jnp.bfloat16)
    far_value = lax.optimization_barrier(far_half).astype(jnp.float32)
    updated = jnp.where(
        keep_tiles[:, None, :, None] == 1,
        jnp.where(near_tiles[:, None, :, None] == 1, near_value, far_value),
        jnp.float32(0.0),
    )
    return (diag_out, factor_out, updated.reshape(trailing.shape))


def solution(mesh):
    in_specs = (
        P("prow", "pcol"),
        P(None, "prow", None, "pcol"),
        P(None, "prow", None, None, "pcol", None),
        P(),
        P(),
        P(),
    )
    out_specs = (
        P("prow", "pcol"),
        P(None, "prow", None, "pcol"),
        P(None, "prow", None, None, "pcol", None),
    )
    return jax.shard_map(
        per_device, mesh=mesh, in_specs=in_specs, out_specs=out_specs, check_vma=False
    )
```

```python
import jax
import jax.numpy as jnp
from jax import lax
from jax.experimental import pallas as pl
from jax.experimental.pallas import tpu as pltpu
from jax.sharding import PartitionSpec as P

BLOCK = 128
PANEL = 16
SUB = 8
FULL = lax.Precision.HIGHEST


def dot_f32(a, b, ca, cb):
    return lax.dot_general(
        a, b, (((ca,), (cb,)), ((), ())), precision=FULL, preferred_element_type=jnp.float32
    )


def factor_block(work):
    sub = lax.broadcasted_iota(jnp.int32, (SUB, BLOCK), 0)
    halves = PANEL // SUB
    for base in range(0, BLOCK, PANEL):
        rows = [work[base + SUB * h : base + SUB * (h + 1), :] for h in range(halves)]
        left = [r[:, :BLOCK] for r in rows]
        right = [r[:, BLOCK:] for r in rows]
        cols = {}
        for k in range(PANEL):
            for h in range(k // SUB, halves):
                cols[k, h] = jnp.broadcast_to(
                    left[h][:, base + k : base + k + 1], (SUB, BLOCK)
                )
        scale = [jnp.ones((SUB, BLOCK), jnp.float32) for _ in range(halves)]
        for m in range(PANEL):
            own, at = m // SUB, m % SUB
            pivot = jnp.broadcast_to(cols[m, own][at : at + 1, :], (SUB, BLOCK))
            root = lax.rsqrt(pivot)
            scale[own] = jnp.where(sub == at, root, scale[own])
            lower = {h: cols[m, h] * root for h in range(own, halves)}
            for k in range(m + 1, PANEL):
                factor = jnp.broadcast_to(
                    lower[k // SUB][k % SUB : k % SUB + 1, :], (SUB, BLOCK)
                )
                for h in range(k // SUB, halves):
                    cols[k, h] = cols[k, h] - lower[h] * factor
            source_left = jnp.broadcast_to(left[own][at : at + 1, :], (SUB, BLOCK)) * root
            source_right = jnp.broadcast_to(right[own][at : at + 1, :], (SUB, BLOCK)) * root
            for h in range(own, halves):
                weight = jnp.where(sub > at, lower[h], 0.0) if h == own else lower[h]
                left[h] = left[h] - weight * source_left
                right[h] = right[h] - weight * source_right
        left = [x * s for x, s in zip(left, scale)]
        right = [x * s for x, s in zip(right, scale)]
        upper = jnp.concatenate(left, 0)
        both = jnp.concatenate([upper, jnp.concatenate(right, 0)], 1)
        work[base : base + PANEL, :] = both
        rest = base + PANEL
        if rest < BLOCK:
            change = dot_f32(upper.T[rest:, :], both, 1, 0)
            work[rest:, :] = work[rest:, :] - change


def cholesky_kernel(gathered, u_ref, v_ref, trail, extra, work):
    width = u_ref.shape[0]
    assemble(gathered, trail, extra)
    u_ref[...] = jnp.zeros_like(u_ref)
    v_ref[...] = jnp.zeros_like(v_ref)
    extra[...] = jnp.zeros_like(extra)
    row = lax.broadcasted_iota(jnp.int32, (BLOCK, BLOCK), 0)
    col = lax.broadcasted_iota(jnp.int32, (BLOCK, BLOCK), 1)
    eye = (row == col).astype(jnp.float32)
    for base in range(0, width, BLOCK):
        here = slice(base, base + BLOCK)
        end = base + BLOCK
        work[:, :BLOCK] = trail[here, here]
        work[:, BLOCK:] = eye
        factor_block(work)
        inverse = work[:, BLOCK:]
        u_ref[here, here] = jnp.where(row <= col, work[:, :BLOCK], 0.0)
        v_ref[here, here] = inverse
        if base:
            v_ref[here, :base] = dot_f32(inverse, extra[here, :base], 1, 0)
        if end < width:
            upper = dot_f32(inverse, trail[here, end:], 1, 0)
            u_ref[here, end:] = upper
            turned = upper.T
            for low in range(end, width, BLOCK):
                piece = turned[low - end : low - end + BLOCK, :]
                trail[low : low + BLOCK, low:] = trail[low : low + BLOCK, low:] - dot_f32(
                    piece, upper[:, low - end :], 1, 0
                )
            extra[end:, :end] = extra[end:, :end] - dot_f32(turned, v_ref[here, :end], 1, 0)


def factorize(a, width):
    shape = jax.ShapeDtypeStruct((width, width), jnp.float32)
    vmem = pl.BlockSpec(memory_space=pltpu.VMEM)
    return pl.pallas_call(
        cholesky_kernel,
        out_shape=(shape, shape),
        in_specs=[vmem],
        out_specs=(vmem, vmem),
        scratch_shapes=[
            pltpu.VMEM((width, width), jnp.float32),
            pltpu.VMEM((width, width), jnp.float32),
            pltpu.VMEM((BLOCK, 2 * BLOCK), jnp.float32),
        ],
        compiler_params=pltpu.CompilerParams(vmem_limit_bytes=32 << 20),
        cost_estimate=pl.CostEstimate(flops=1 << 32, bytes_accessed=4 << 20, transcendentals=0),
        name="factorize",
    )(a)


def split(x):
    high = x.astype(jnp.bfloat16)
    return high, (x - high.astype(jnp.float32)).astype(jnp.bfloat16)


def assemble(gathered, a_ref, direct):
    count, width = gathered.shape[0], a_ref.shape[0]
    side = width // count
    per = BLOCK // side
    lane = lax.broadcasted_iota(jnp.int32, (SUB, BLOCK), 1) // side
    for q in range(count):
        held = {}
        for o in range(count // 2 + 1):
            if o < count // 2 or q < count // 2:
                held[(q + o) % count] = gathered[q, o]
        for g in range(side // SUB):
            for tile in range(count // per):
                total = jnp.zeros((SUB, BLOCK), jnp.float32)
                for e in range(per):
                    piece = held.get(tile * per + e)
                    if piece is not None:
                        shift = (e - g) % per * side
                        moved = pltpu.roll(piece, shift, 1) if shift else piece
                        total = jnp.where(lane == e, moved, total)
                low = q * side + g * SUB
                direct[low : low + SUB, tile * BLOCK : (tile + 1) * BLOCK] = total
    row = lax.broadcasted_iota(jnp.int32, (BLOCK, BLOCK), 0) // side
    col = lax.broadcasted_iota(jnp.int32, (BLOCK, BLOCK), 1) // side
    for i in range(0, width, BLOCK):
        for j in range(i, width, BLOCK):
            here = direct[i : i + BLOCK, j : j + BLOCK]
            there = direct[j : j + BLOCK, i : i + BLOCK].T
            if i == j:
                there = jnp.where(row == col, 0.0, there)
            a_ref[i : i + BLOCK, j : j + BLOCK] = here + there


def update_kernel(
    kept, near, scale, u_ref, v_ref, rows_ref, cols_ref, trailing, out_hbm, factor_ref, diag_ref,
    current, result, srow, frow_h, frow_l, scol_h, scol_l, turned, sems,
):
    tiles, pieces, side, width = rows_ref.shape
    p, q = lax.axis_index("prow"), lax.axis_index("pcol")
    rows_all = lax.axis_size("prow")
    cols_all = lax.axis_size("pcol")
    half = current.shape[0] // tiles
    chunks = width // BLOCK
    loads = [
        pltpu.make_async_copy(
            trailing.at[pl.ds(r * half, half)], current.at[pl.ds(r * half, half)], sems.at[r]
        )
        for r in range(tiles)
    ]
    for load in loads:
        load.start()
    turned[...] = u_ref[pl.ds(pl.multiple_of(q * side, side), side), :].T
    diag_ref[...] = turned[pl.ds(pl.multiple_of(p * side, side), side), :]
    mid = width // 2

    def solve(piece):
        top = dot_f32(v_ref[:mid, :mid], piece[:mid, :], 1, 0)
        low = dot_f32(v_ref[mid:, :], piece, 1, 0)
        return jnp.concatenate([top, low], 0)

    for r in range(tiles):
        keep = kept[r * rows_all + p + 1, 0].astype(jnp.float32)
        solved = solve(rows_ref[r].reshape(width, width)) * keep
        srow[r] = solved
        high, low = split(solved.T)
        frow_h[r] = high
        frow_l[r] = low
    for t in range(tiles):
        keep = kept[t * cols_all + q + 1, 0].astype(jnp.float32)
        high, low = split(solve(cols_ref[t].reshape(width, width)) * keep)
        scol_h[t] = high
        scol_l[t] = low
    for r in range(tiles):
        factor_ref[r] = srow[r, pl.ds(pl.multiple_of(q * side, side), side), :]

    def dot_half(a, b):
        return jnp.dot(a, b, preferred_element_type=jnp.float32)

    stores = []
    for r in range(tiles):
        loads[r].wait()
        for t in range(tiles):
            i, j = r * rows_all + p + 1, t * cols_all + q + 1
            is_kept = kept[i, j] == 1
            is_near = near[i, j] == 1

            def place(l):
                return pl.ds(r * half + t * chunks + l, width, stride=tiles * chunks)

            @pl.when(jnp.logical_and(is_kept, is_near))
            def _():
                exact = dot_half(frow_h[r], scol_h[t]) + (
                    dot_half(frow_h[r], scol_l[t]) + dot_half(frow_l[r], scol_h[t])
                )
                for l in range(chunks):
                    result[place(l), :] = (
                        current[place(l), :] - exact[:, l * BLOCK : (l + 1) * BLOCK]
                    )

            @pl.when(jnp.logical_and(is_kept, jnp.logical_not(is_near)))
            def _():
                rough = dot_half(frow_h[r], scol_h[t]) / scale[i, j]
                for l in range(chunks):
                    far = current[place(l), :] - rough[:, l * BLOCK : (l + 1) * BLOCK]
                    result[place(l), :] = far.astype(jnp.bfloat16).astype(jnp.float32)

            @pl.when(jnp.logical_not(is_kept))
            def _():
                for l in range(chunks):
                    result[place(l), :] = jnp.zeros((width, BLOCK), jnp.float32)

        store = pltpu.make_async_copy(
            result.at[pl.ds(r * half, half)], out_hbm.at[pl.ds(r * half, half)], sems.at[tiles + r]
        )
        store.start()
        stores.append(store)
    for store in stores:
        store.wait()


def update(kept, near, scale, upper, inverse, rows, cols, trailing):
    tiles, pieces, side, width = rows.shape
    vmem = pl.BlockSpec(memory_space=pltpu.VMEM)
    smem = pl.BlockSpec(memory_space=pltpu.SMEM)
    hbm = pl.BlockSpec(memory_space=pl.ANY)
    flat = trailing.reshape(trailing.size // BLOCK, BLOCK)
    shape = jax.ShapeDtypeStruct
    return pl.pallas_call(
        update_kernel,
        out_shape=(
            shape(flat.shape, jnp.float32),
            shape((tiles, side, width), jnp.float32),
            shape((side, side), jnp.float32),
        ),
        in_specs=[smem, smem, smem, vmem, vmem, vmem, vmem, hbm],
        out_specs=(hbm, vmem, vmem),
        scratch_shapes=[
            pltpu.VMEM(flat.shape, jnp.float32),
            pltpu.VMEM(flat.shape, jnp.float32),
            pltpu.VMEM((tiles, width, width), jnp.float32),
            pltpu.VMEM((tiles, width, width), jnp.bfloat16),
            pltpu.VMEM((tiles, width, width), jnp.bfloat16),
            pltpu.VMEM((tiles, width, width), jnp.bfloat16),
            pltpu.VMEM((tiles, width, width), jnp.bfloat16),
            pltpu.VMEM((width, side), jnp.float32),
            pltpu.SemaphoreType.DMA((2 * tiles,)),
        ],
        compiler_params=pltpu.CompilerParams(vmem_limit_bytes=56 << 20),
        name="update",
    )(kept, near, scale, upper, inverse, rows, cols, flat)


def exchange_kernel(
    pack, own, gathered, rows, cols, first, turned,
    local_sems, turn_sems, send1, recv1, send2, recv2, send3, recv3, send4, recv4,
):
    p, q = lax.axis_index("prow"), lax.axis_index("pcol")
    n, m = lax.axis_size("prow"), lax.axis_size("pcol")
    keep = gathered.shape[1]
    mesh_id = pl.DeviceIdType.MESH

    def others(me, count, body):
        def step(s, carry):
            body(lax.rem(me + s, count))
            return carry

        lax.fori_loop(1, count, step, 0)

    barrier = pltpu.get_barrier_semaphore()

    def greet(a, b):
        pl.semaphore_signal(barrier, inc=1, device_id=(a, b), device_id_type=mesh_id)

    others(p, n, lambda a: greet(a, q))
    others(q, m, lambda b: greet(p, b))

    @pl.when(p != q)
    def _():
        greet(q, p)

    pl.semaphore_wait(barrier, n + m - 2 + (p != q).astype(jnp.int32))

    def remote(src, dst, send, recv, a, b):
        return pltpu.make_async_remote_copy(
            src_ref=src, dst_ref=dst, send_sem=send, recv_sem=recv,
            device_id=(a, b), device_id_type=mesh_id,
        )

    slot = lax.rem(p + m - q, m)
    mine = pltpu.make_async_copy(pack, first.at[slot], local_sems.at[0])
    mine.start()

    def first_copy(a, sender):
        at = lax.rem(sender + m - q, m)
        return remote(pack, first.at[at], send1.at[a], recv1.at[sender], a, q)

    others(p, n, lambda a: first_copy(a, p).start())

    swap = remote(own, turned, turn_sems.at[0], turn_sems.at[1], q, p)
    stay = pltpu.make_async_copy(own, turned, local_sems.at[1])

    @pl.when(p != q)
    def _():
        swap.start()

    @pl.when(p == q)
    def _():
        stay.start()

    mine.wait()
    others(p, n, lambda a: first_copy(a, a).wait_recv())

    part = first.at[pl.ds(0, keep)]
    block = pltpu.make_async_copy(part, gathered.at[q], local_sems.at[2])
    block.start()

    def second_copy(b, sender):
        return remote(part, gathered.at[sender], send2.at[b], recv2.at[sender], p, b)

    others(q, m, lambda b: second_copy(b, q).start())

    @pl.when(p != q)
    def _():
        swap.wait()

    @pl.when(p == q)
    def _():
        stay.wait()

    core = lax.rem(p, 2)
    other = p + 1 - 2 * core
    held = pltpu.make_async_copy(turned.at[core], cols.at[core, p], local_sems.at[3])
    held.start()

    def fourth_copy(a, sender, tile):
        return remote(
            turned.at[tile], cols.at[tile, sender], send4.at[a], recv4.at[sender], a, q
        )

    others(p, n, lambda a: fourth_copy(a, p, lax.rem(a, 2)).start())

    block.wait()
    others(q, m, lambda b: second_copy(b, b).wait_recv())

    whole = pltpu.make_async_copy(own, rows.at[:, q], local_sems.at[4])
    whole.start()

    def third_copy(b, sender):
        return remote(own, rows.at[:, sender], send3.at[b], recv3.at[sender], p, b)

    others(q, m, lambda b: third_copy(b, q).start())

    held.wait()
    others(p, n, lambda a: fourth_copy(a, a, core).wait_recv())
    partner = remote(cols.at[core], cols.at[core], turn_sems.at[2], turn_sems.at[3], other, q)
    partner.start()
    whole.wait()
    others(q, m, lambda b: third_copy(b, b).wait_recv())
    partner.wait()
    others(p, n, lambda a: first_copy(a, p).wait_send())
    others(q, m, lambda b: second_copy(b, q).wait_send())
    others(q, m, lambda b: third_copy(b, q).wait_send())
    others(p, n, lambda a: fourth_copy(a, p, lax.rem(a, 2)).wait_send())


def exchange(pack, own):
    n, m = lax.axis_size("prow"), lax.axis_size("pcol")
    tiles, side, width = own.shape
    vmem = pl.BlockSpec(memory_space=pltpu.VMEM)
    shape = jax.ShapeDtypeStruct
    dma = pltpu.SemaphoreType.DMA
    return pl.pallas_call(
        exchange_kernel,
        out_shape=(
            shape((m, n // 2 + 1, SUB, BLOCK), jnp.float32),
            shape((tiles, m, side, width), jnp.float32),
            shape((tiles, n, side, width), jnp.float32),
        ),
        in_specs=[vmem, vmem],
        out_specs=(vmem, vmem, vmem),
        scratch_shapes=[
            pltpu.VMEM((n, SUB, BLOCK), jnp.float32),
            pltpu.VMEM((tiles, side, width), jnp.float32),
            dma((5,)), dma((4,)),
            dma((n,)), dma((n,)), dma((m,)), dma((m,)),
            dma((m,)), dma((m,)), dma((n,)), dma((n,)),
        ],
        compiler_params=pltpu.CompilerParams(
            collective_id=0, has_side_effects=True, vmem_limit_bytes=32 << 20
        ),
        name="exchange",
    )(pack, own)


def per_device(diag_tile, panel, trailing, kept, precision, tile_scale):
    side = diag_tile.shape[0]
    own = jnp.transpose(panel[:, 0], (0, 2, 1))
    pack = diag_tile.T.reshape(side // SUB, SUB, side).transpose(1, 0, 2).reshape(SUB, BLOCK)
    gathered, rows, cols = exchange(pack, own)
    upper, inverse = factorize(gathered, panel.shape[2])
    updated, factor, diag_out = update(
        kept, precision, tile_scale, upper, inverse, rows, cols, trailing
    )
    factor_out = jnp.transpose(factor, (0, 2, 1))[:, None]
    return (diag_out, factor_out, updated.reshape(trailing.shape))


def solution(mesh):
    in_specs = (
        P("prow", "pcol"),
        P(None, "prow", None, "pcol"),
        P(None, "prow", None, None, "pcol", None),
        P(),
        P(),
        P(),
    )
    out_specs = (
        P("prow", "pcol"),
        P(None, "prow", None, "pcol"),
        P(None, "prow", None, None, "pcol", None),
    )
    return jax.shard_map(
        per_device, mesh=mesh, in_specs=in_specs, out_specs=out_specs, check_vma=False
    )
```

```python
import jax
import jax.numpy as jnp
from jax import lax
from jax.experimental import pallas as pl
from jax.experimental.pallas import tpu as pltpu
from jax.sharding import PartitionSpec as P

BLOCK = 128
PANEL = 16
SUB = 8
FULL = lax.Precision.HIGHEST


def dot_f32(a, b, ca, cb):
    return lax.dot_general(
        a, b, (((ca,), (cb,)), ((), ())), precision=FULL, preferred_element_type=jnp.float32
    )


def factor_block(work):
    sub = lax.broadcasted_iota(jnp.int32, (SUB, BLOCK), 0)
    halves = PANEL // SUB
    for base in range(0, BLOCK, PANEL):
        rows = [work[base + SUB * h : base + SUB * (h + 1), :] for h in range(halves)]
        left = [r[:, :BLOCK] for r in rows]
        right = [r[:, BLOCK:] for r in rows]
        cols = {}
        for k in range(PANEL):
            for h in range(k // SUB, halves):
                cols[k, h] = jnp.broadcast_to(
                    left[h][:, base + k : base + k + 1], (SUB, BLOCK)
                )
        scale = [jnp.ones((SUB, BLOCK), jnp.float32) for _ in range(halves)]
        for m in range(PANEL):
            own, at = m // SUB, m % SUB
            pivot = jnp.broadcast_to(cols[m, own][at : at + 1, :], (SUB, BLOCK))
            root = lax.rsqrt(pivot)
            scale[own] = jnp.where(sub == at, root, scale[own])
            lower = {h: cols[m, h] * root for h in range(own, halves)}
            for k in range(m + 1, PANEL):
                factor = jnp.broadcast_to(
                    lower[k // SUB][k % SUB : k % SUB + 1, :], (SUB, BLOCK)
                )
                for h in range(k // SUB, halves):
                    cols[k, h] = cols[k, h] - lower[h] * factor
            source_left = jnp.broadcast_to(left[own][at : at + 1, :], (SUB, BLOCK)) * root
            source_right = jnp.broadcast_to(right[own][at : at + 1, :], (SUB, BLOCK)) * root
            for h in range(own, halves):
                weight = jnp.where(sub > at, lower[h], 0.0) if h == own else lower[h]
                left[h] = left[h] - weight * source_left
                right[h] = right[h] - weight * source_right
        left = [x * s for x, s in zip(left, scale)]
        right = [x * s for x, s in zip(right, scale)]
        upper = jnp.concatenate(left, 0)
        both = jnp.concatenate([upper, jnp.concatenate(right, 0)], 1)
        work[base : base + PANEL, :] = both
        rest = base + PANEL
        if rest < BLOCK:
            change = dot_f32(upper.T[rest:, :], both, 1, 0)
            work[rest:, :] = work[rest:, :] - change


def cholesky_kernel(gathered, u_ref, v_ref, trail, extra, work):
    width = u_ref.shape[0]
    assemble(gathered, trail, extra)
    u_ref[...] = jnp.zeros_like(u_ref)
    v_ref[...] = jnp.zeros_like(v_ref)
    extra[...] = jnp.zeros_like(extra)
    row = lax.broadcasted_iota(jnp.int32, (BLOCK, BLOCK), 0)
    col = lax.broadcasted_iota(jnp.int32, (BLOCK, BLOCK), 1)
    eye = (row == col).astype(jnp.float32)
    for base in range(0, width, BLOCK):
        here = slice(base, base + BLOCK)
        end = base + BLOCK
        work[:, :BLOCK] = trail[here, here]
        work[:, BLOCK:] = eye
        factor_block(work)
        inverse = work[:, BLOCK:]
        u_ref[here, here] = jnp.where(row <= col, work[:, :BLOCK], 0.0)
        v_ref[here, here] = inverse
        if base:
            v_ref[here, :base] = dot_f32(inverse, extra[here, :base], 1, 0)
        if end < width:
            upper = dot_f32(inverse, trail[here, end:], 1, 0)
            u_ref[here, end:] = upper
            turned = upper.T
            for low in range(end, width, BLOCK):
                piece = turned[low - end : low - end + BLOCK, :]
                trail[low : low + BLOCK, low:] = trail[low : low + BLOCK, low:] - dot_f32(
                    piece, upper[:, low - end :], 1, 0
                )
            extra[end:, :end] = extra[end:, :end] - dot_f32(turned, v_ref[here, :end], 1, 0)


def split(x):
    high = x.astype(jnp.bfloat16)
    return high, (x - high.astype(jnp.float32)).astype(jnp.bfloat16)


def assemble(gathered, a_ref, direct):
    count, width = gathered.shape[0], a_ref.shape[0]
    side = width // count
    per = BLOCK // side
    lane = lax.broadcasted_iota(jnp.int32, (SUB, BLOCK), 1) // side
    for q in range(count):
        held = {}
        for o in range(count // 2 + 1):
            if o < count // 2 or q < count // 2:
                held[(q + o) % count] = gathered[q, o]
        for g in range(side // SUB):
            for tile in range(count // per):
                total = jnp.zeros((SUB, BLOCK), jnp.float32)
                for e in range(per):
                    piece = held.get(tile * per + e)
                    if piece is not None:
                        shift = (e - g) % per * side
                        moved = pltpu.roll(piece, shift, 1) if shift else piece
                        total = jnp.where(lane == e, moved, total)
                low = q * side + g * SUB
                direct[low : low + SUB, tile * BLOCK : (tile + 1) * BLOCK] = total
    row = lax.broadcasted_iota(jnp.int32, (BLOCK, BLOCK), 0) // side
    col = lax.broadcasted_iota(jnp.int32, (BLOCK, BLOCK), 1) // side
    for i in range(0, width, BLOCK):
        for j in range(i, width, BLOCK):
            here = direct[i : i + BLOCK, j : j + BLOCK]
            there = direct[j : j + BLOCK, i : i + BLOCK].T
            if i == j:
                there = jnp.where(row == col, 0.0, there)
            a_ref[i : i + BLOCK, j : j + BLOCK] = here + there


def update_kernel(
    kept, near, scale, u_ref, v_ref, rows_ref, cols_ref, trailing, out_hbm, factor_ref, diag_ref,
    current, result, srow, frow_h, frow_l, scol_h, scol_l, turned, sems,
):
    tiles, pieces, side, width = rows_ref.shape
    p, q = lax.axis_index("prow"), lax.axis_index("pcol")
    rows_all = lax.axis_size("prow")
    cols_all = lax.axis_size("pcol")
    half = current.shape[0] // tiles
    chunks = width // BLOCK
    loads = [
        pltpu.make_async_copy(
            trailing.at[pl.ds(r * half, half)], current.at[pl.ds(r * half, half)], sems.at[r]
        )
        for r in range(tiles)
    ]
    for load in loads:
        load.start()
    turned[...] = u_ref[pl.ds(pl.multiple_of(q * side, side), side), :].T
    diag_ref[...] = turned[pl.ds(pl.multiple_of(p * side, side), side), :]
    mid = width // 2

    def solve(piece):
        top = dot_f32(v_ref[:mid, :mid], piece[:mid, :], 1, 0)
        low = dot_f32(v_ref[mid:, :], piece, 1, 0)
        return jnp.concatenate([top, low], 0)

    for r in range(tiles):
        keep = kept[r * rows_all + p + 1, 0].astype(jnp.float32)
        solved = solve(rows_ref[r].reshape(width, width)) * keep
        srow[r] = solved
        high, low = split(solved.T)
        frow_h[r] = high
        frow_l[r] = low
    for t in range(tiles):
        keep = kept[t * cols_all + q + 1, 0].astype(jnp.float32)
        high, low = split(solve(cols_ref[t].reshape(width, width)) * keep)
        scol_h[t] = high
        scol_l[t] = low
    for r in range(tiles):
        factor_ref[r] = srow[r, pl.ds(pl.multiple_of(q * side, side), side), :]

    def dot_half(a, b):
        return jnp.dot(a, b, preferred_element_type=jnp.float32)

    stores = []
    for r in range(tiles):
        loads[r].wait()
        for t in range(tiles):
            i, j = r * rows_all + p + 1, t * cols_all + q + 1
            is_kept = kept[i, j] == 1
            is_near = near[i, j] == 1

            def place(l):
                return pl.ds(r * half + t * chunks + l, width, stride=tiles * chunks)

            @pl.when(jnp.logical_and(is_kept, is_near))
            def _():
                exact = dot_half(frow_h[r], scol_h[t]) + (
                    dot_half(frow_h[r], scol_l[t]) + dot_half(frow_l[r], scol_h[t])
                )
                for l in range(chunks):
                    result[place(l), :] = (
                        current[place(l), :] - exact[:, l * BLOCK : (l + 1) * BLOCK]
                    )

            @pl.when(jnp.logical_and(is_kept, jnp.logical_not(is_near)))
            def _():
                rough = dot_half(frow_h[r], scol_h[t]) / scale[i, j]
                for l in range(chunks):
                    far = current[place(l), :] - rough[:, l * BLOCK : (l + 1) * BLOCK]
                    result[place(l), :] = far.astype(jnp.bfloat16).astype(jnp.float32)

            @pl.when(jnp.logical_not(is_kept))
            def _():
                for l in range(chunks):
                    result[place(l), :] = jnp.zeros((width, BLOCK), jnp.float32)

        store = pltpu.make_async_copy(
            result.at[pl.ds(r * half, half)], out_hbm.at[pl.ds(r * half, half)], sems.at[tiles + r]
        )
        store.start()
        stores.append(store)
    for store in stores:
        store.wait()


def update(kept, near, scale, upper, inverse, rows, cols, trailing):
    tiles, pieces, side, width = rows.shape
    vmem = pl.BlockSpec(memory_space=pltpu.VMEM)
    smem = pl.BlockSpec(memory_space=pltpu.SMEM)
    hbm = pl.BlockSpec(memory_space=pltpu.HBM)
    flat = trailing.reshape(trailing.size // BLOCK, BLOCK)
    shape = jax.ShapeDtypeStruct
    return pl.pallas_call(
        update_kernel,
        out_shape=(
            shape(flat.shape, jnp.float32),
            shape((tiles, side, width), jnp.float32),
            shape((side, side), jnp.float32),
        ),
        in_specs=[smem, smem, smem, vmem, vmem, vmem, vmem, hbm],
        out_specs=(hbm, vmem, vmem),
        scratch_shapes=[
            pltpu.VMEM(flat.shape, jnp.float32),
            pltpu.VMEM(flat.shape, jnp.float32),
            pltpu.VMEM((tiles, width, width), jnp.float32),
            pltpu.VMEM((tiles, width, width), jnp.bfloat16),
            pltpu.VMEM((tiles, width, width), jnp.bfloat16),
            pltpu.VMEM((tiles, width, width), jnp.bfloat16),
            pltpu.VMEM((tiles, width, width), jnp.bfloat16),
            pltpu.VMEM((width, side), jnp.float32),
            pltpu.SemaphoreType.DMA((2 * tiles,)),
        ],
        compiler_params=pltpu.CompilerParams(vmem_limit_bytes=45 << 20),
        name="update",
    )(kept, near, scale, upper, inverse, rows, cols, flat)


def panel_kernel(
    pack, own, upper, inverse, rows, cols, gathered, first, turned, trail, extra, work,
    local_sems, turn_sems, send1, recv1, send2, recv2, send3, recv3, send4, recv4,
):
    p, q = lax.axis_index("prow"), lax.axis_index("pcol")
    n, m = lax.axis_size("prow"), lax.axis_size("pcol")
    keep = gathered.shape[1]
    mesh_id = pl.DeviceIdType.MESH

    def others(me, count, body):
        def step(s, carry):
            body(lax.rem(me + s, count))
            return carry

        lax.fori_loop(1, count, step, 0)

    barrier = pltpu.get_barrier_semaphore()

    def greet(a, b):
        pl.semaphore_signal(barrier, inc=1, device_id=(a, b), device_id_type=mesh_id)

    others(p, n, lambda a: greet(a, q))
    others(q, m, lambda b: greet(p, b))

    @pl.when(p != q)
    def _():
        greet(q, p)

    pl.semaphore_wait(barrier, n + m - 2 + (p != q).astype(jnp.int32))

    def remote(src, dst, send, recv, a, b):
        return pltpu.make_async_remote_copy(
            src_ref=src, dst_ref=dst, send_sem=send, recv_sem=recv,
            device_id=(a, b), device_id_type=mesh_id,
        )

    slot = lax.rem(p + m - q, m)
    mine = pltpu.make_async_copy(pack, first.at[slot], local_sems.at[0])
    mine.start()

    def first_copy(a, sender):
        at = lax.rem(sender + m - q, m)
        return remote(pack, first.at[at], send1.at[a], recv1.at[sender], a, q)

    others(p, n, lambda a: first_copy(a, p).start())

    swap = remote(own, turned, turn_sems.at[0], turn_sems.at[1], q, p)
    stay = pltpu.make_async_copy(own, turned, local_sems.at[1])

    @pl.when(p != q)
    def _():
        swap.start()

    @pl.when(p == q)
    def _():
        stay.start()

    mine.wait()
    others(p, n, lambda a: first_copy(a, a).wait_recv())

    part = first.at[pl.ds(0, keep)]
    block = pltpu.make_async_copy(part, gathered.at[q], local_sems.at[2])
    block.start()

    def second_copy(b, sender):
        return remote(part, gathered.at[sender], send2.at[b], recv2.at[sender], p, b)

    others(q, m, lambda b: second_copy(b, q).start())

    @pl.when(p != q)
    def _():
        swap.wait()

    @pl.when(p == q)
    def _():
        stay.wait()

    core = lax.rem(p, 2)
    other = p + 1 - 2 * core
    held = pltpu.make_async_copy(turned.at[core], cols.at[core, p], local_sems.at[3])
    held.start()

    def fourth_copy(a, sender, tile):
        return remote(
            turned.at[tile], cols.at[tile, sender], send4.at[a], recv4.at[sender], a, q
        )

    others(p, n, lambda a: fourth_copy(a, p, lax.rem(a, 2)).start())

    block.wait()
    others(q, m, lambda b: second_copy(b, b).wait_recv())

    whole = pltpu.make_async_copy(own, rows.at[:, q], local_sems.at[4])
    whole.start()

    def third_copy(b, sender):
        return remote(own, rows.at[:, sender], send3.at[b], recv3.at[sender], p, b)

    others(q, m, lambda b: third_copy(b, q).start())

    cholesky_kernel(gathered, upper, inverse, trail, extra, work)

    held.wait()
    others(p, n, lambda a: fourth_copy(a, a, core).wait_recv())
    partner = remote(cols.at[core], cols.at[core], turn_sems.at[2], turn_sems.at[3], other, q)
    partner.start()
    whole.wait()
    others(q, m, lambda b: third_copy(b, b).wait_recv())
    partner.wait()
    others(p, n, lambda a: first_copy(a, p).wait_send())
    others(q, m, lambda b: second_copy(b, q).wait_send())
    others(q, m, lambda b: third_copy(b, q).wait_send())
    others(p, n, lambda a: fourth_copy(a, p, lax.rem(a, 2)).wait_send())


def panel_step(pack, own):
    n, m = lax.axis_size("prow"), lax.axis_size("pcol")
    tiles, side, width = own.shape
    vmem = pl.BlockSpec(memory_space=pltpu.VMEM)
    shape = jax.ShapeDtypeStruct
    dma = pltpu.SemaphoreType.DMA
    return pl.pallas_call(
        panel_kernel,
        out_shape=(
            shape((width, width), jnp.float32),
            shape((width, width), jnp.float32),
            shape((tiles, m, side, width), jnp.float32),
            shape((tiles, n, side, width), jnp.float32),
        ),
        in_specs=[vmem, vmem],
        out_specs=(vmem, vmem, vmem, vmem),
        scratch_shapes=[
            pltpu.VMEM((m, n // 2 + 1, SUB, BLOCK), jnp.float32),
            pltpu.VMEM((n, SUB, BLOCK), jnp.float32),
            pltpu.VMEM((tiles, side, width), jnp.float32),
            pltpu.VMEM((width, width), jnp.float32),
            pltpu.VMEM((width, width), jnp.float32),
            pltpu.VMEM((BLOCK, 2 * BLOCK), jnp.float32),
            dma((5,)), dma((4,)),
            dma((n,)), dma((n,)), dma((m,)), dma((m,)),
            dma((m,)), dma((m,)), dma((n,)), dma((n,)),
        ],
        compiler_params=pltpu.CompilerParams(
            collective_id=0, has_side_effects=True, vmem_limit_bytes=32 << 20
        ),
        name="panel",
    )(pack, own)


def per_device(diag_tile, panel, trailing, kept, precision, tile_scale):
    side = diag_tile.shape[0]
    own = jnp.transpose(panel[:, 0], (0, 2, 1))
    pack = diag_tile.T.reshape(side // SUB, SUB, side).transpose(1, 0, 2).reshape(SUB, BLOCK)
    upper, inverse, rows, cols = panel_step(pack, own)
    updated, factor, diag_out = update(
        kept, precision, tile_scale, upper, inverse, rows, cols, trailing
    )
    factor_out = jnp.transpose(factor, (0, 2, 1))[:, None]
    return (diag_out, factor_out, updated.reshape(trailing.shape))


def solution(mesh):
    in_specs = (
        P("prow", "pcol"),
        P(None, "prow", None, "pcol"),
        P(None, "prow", None, None, "pcol", None),
        P(),
        P(),
        P(),
    )
    out_specs = (
        P("prow", "pcol"),
        P(None, "prow", None, "pcol"),
        P(None, "prow", None, None, "pcol", None),
    )
    return jax.shard_map(
        per_device, mesh=mesh, in_specs=in_specs, out_specs=out_specs, check_vma=False
    )
```

```python
import jax
import jax.numpy as jnp
from jax import lax
from jax.experimental import pallas as pl
from jax.experimental.pallas import tpu as pltpu
from jax.sharding import PartitionSpec as P

BLOCK = 128
PANEL = 16
SUB = 8
ACROSS = 4
FULL = lax.Precision.HIGHEST


def dot_f32(a, b, ca, cb):
    return lax.dot_general(
        a, b, (((ca,), (cb,)), ((), ())), precision=FULL, preferred_element_type=jnp.float32
    )


def factor_block(work):
    sub = lax.broadcasted_iota(jnp.int32, (SUB, BLOCK), 0)
    halves = PANEL // SUB
    for base in range(0, BLOCK, PANEL):
        rows = [work[base + SUB * h : base + SUB * (h + 1), :] for h in range(halves)]
        left = [r[:, :BLOCK] for r in rows]
        right = [r[:, BLOCK:] for r in rows]
        cols = {}
        for k in range(PANEL):
            for h in range(k // SUB, halves):
                cols[k, h] = jnp.broadcast_to(
                    left[h][:, base + k : base + k + 1], (SUB, BLOCK)
                )
        scale = [jnp.ones((SUB, BLOCK), jnp.float32) for _ in range(halves)]
        for m in range(PANEL):
            own, at = m // SUB, m % SUB
            pivot = jnp.broadcast_to(cols[m, own][at : at + 1, :], (SUB, BLOCK))
            root = lax.rsqrt(pivot)
            scale[own] = jnp.where(sub == at, root, scale[own])
            lower = {h: cols[m, h] * root for h in range(own, halves)}
            for k in range(m + 1, PANEL):
                factor = jnp.broadcast_to(
                    lower[k // SUB][k % SUB : k % SUB + 1, :], (SUB, BLOCK)
                )
                for h in range(k // SUB, halves):
                    cols[k, h] = cols[k, h] - lower[h] * factor
            source_left = jnp.broadcast_to(left[own][at : at + 1, :], (SUB, BLOCK)) * root
            source_right = jnp.broadcast_to(right[own][at : at + 1, :], (SUB, BLOCK)) * root
            for h in range(own, halves):
                weight = jnp.where(sub > at, lower[h], 0.0) if h == own else lower[h]
                left[h] = left[h] - weight * source_left
                right[h] = right[h] - weight * source_right
        left = [x * s for x, s in zip(left, scale)]
        right = [x * s for x, s in zip(right, scale)]
        upper = jnp.concatenate(left, 0)
        both = jnp.concatenate([upper, jnp.concatenate(right, 0)], 1)
        work[base : base + PANEL, :] = both
        rest = base + PANEL
        if rest < BLOCK:
            change = dot_f32(upper.T[rest:, :], both, 1, 0)
            work[rest:, :] = work[rest:, :] - change


def cholesky_kernel(gathered, u_ref, v_ref, trail, extra, work, between):
    width = u_ref.shape[0]
    assemble(gathered, trail, extra)
    u_ref[...] = jnp.zeros_like(u_ref)
    v_ref[...] = jnp.zeros_like(v_ref)
    extra[...] = jnp.zeros_like(extra)
    row = lax.broadcasted_iota(jnp.int32, (BLOCK, BLOCK), 0)
    col = lax.broadcasted_iota(jnp.int32, (BLOCK, BLOCK), 1)
    eye = (row == col).astype(jnp.float32)
    for base in range(0, width, BLOCK):
        here = slice(base, base + BLOCK)
        end = base + BLOCK
        work[:, :BLOCK] = trail[here, here]
        work[:, BLOCK:] = eye
        factor_block(work)
        if base == 0:
            between()
        inverse = work[:, BLOCK:]
        u_ref[here, here] = jnp.where(row <= col, work[:, :BLOCK], 0.0)
        v_ref[here, here] = inverse
        if base:
            v_ref[here, :base] = dot_f32(inverse, extra[here, :base], 1, 0)
        if end < width:
            upper = dot_f32(inverse, trail[here, end:], 1, 0)
            u_ref[here, end:] = upper
            turned = upper.T
            for low in range(end, width, BLOCK):
                piece = turned[low - end : low - end + BLOCK, :]
                trail[low : low + BLOCK, low:] = trail[low : low + BLOCK, low:] - dot_f32(
                    piece, upper[:, low - end :], 1, 0
                )
            extra[end:, :end] = extra[end:, :end] - dot_f32(turned, v_ref[here, :end], 1, 0)


def split(x):
    high = x.astype(jnp.bfloat16)
    return high, (x - high.astype(jnp.float32)).astype(jnp.bfloat16)


def assemble(gathered, a_ref, direct):
    count, width = gathered.shape[0], a_ref.shape[0]
    side = width // count
    per = BLOCK // side
    lane = lax.broadcasted_iota(jnp.int32, (SUB, BLOCK), 1) // side
    for q in range(count):
        held = {}
        for o in range(count // 2 + 1):
            if o < count // 2 or q < count // 2:
                held[(q + o) % count] = gathered[q, o]
        for g in range(side // SUB):
            for tile in range(count // per):
                total = jnp.zeros((SUB, BLOCK), jnp.float32)
                for e in range(per):
                    piece = held.get(tile * per + e)
                    if piece is not None:
                        shift = (e - g) % per * side
                        moved = pltpu.roll(piece, shift, 1) if shift else piece
                        total = jnp.where(lane == e, moved, total)
                low = q * side + g * SUB
                direct[low : low + SUB, tile * BLOCK : (tile + 1) * BLOCK] = total
    row = lax.broadcasted_iota(jnp.int32, (BLOCK, BLOCK), 0) // side
    col = lax.broadcasted_iota(jnp.int32, (BLOCK, BLOCK), 1) // side
    for i in range(0, width, BLOCK):
        for j in range(i, width, BLOCK):
            here = direct[i : i + BLOCK, j : j + BLOCK]
            there = direct[j : j + BLOCK, i : i + BLOCK].T
            if i == j:
                there = jnp.where(row == col, 0.0, there)
            a_ref[i : i + BLOCK, j : j + BLOCK] = here + there


def update_kernel(
    kept, near, scale, u_ref, v_ref, rows_ref, cols_ref, trailing, out_hbm, factor_ref, diag_ref,
    current, result, srow, frow_h, frow_l, scol_h, scol_l, turned, sems,
):
    tiles, pieces, side, width = cols_ref.shape
    p, q = lax.axis_index("prow"), lax.axis_index("pcol")
    rows_all = lax.axis_size("prow")
    cols_all = lax.axis_size("pcol")
    half = current.shape[0] // tiles
    chunks = width // BLOCK
    loads = [
        pltpu.make_async_copy(
            trailing.at[pl.ds(r * half, half)], current.at[pl.ds(r * half, half)], sems.at[r]
        )
        for r in range(tiles)
    ]
    for load in loads:
        load.start()
    turned[...] = u_ref[pl.ds(pl.multiple_of(q * side, side), side), :].T
    diag_ref[...] = turned[pl.ds(pl.multiple_of(p * side, side), side), :]
    mid = width // 2

    def solve(piece):
        top = dot_f32(v_ref[:mid, :mid], piece[:mid, :], 1, 0)
        low = dot_f32(v_ref[mid:, :], piece, 1, 0)
        return jnp.concatenate([top, low], 0)

    for r in range(tiles):
        keep = kept[r * rows_all + p + 1, 0].astype(jnp.float32)
        solved = solve(rows_ref[r].reshape(width, width)) * keep
        srow[r] = solved
        high, low = split(solved.T)
        frow_h[r] = high
        frow_l[r] = low
    for t in range(tiles):
        keep = kept[t * cols_all + q + 1, 0].astype(jnp.float32)
        high, low = split(solve(cols_ref[t].reshape(width, width)) * keep)
        scol_h[t] = high
        scol_l[t] = low
    for r in range(tiles):
        factor_ref[r] = srow[r, pl.ds(pl.multiple_of(q * side, side), side), :]

    def dot_half(a, b):
        return jnp.dot(a, b, preferred_element_type=jnp.float32)

    stores = []
    for r in range(tiles):
        loads[r].wait()
        for t in range(tiles):
            i, j = r * rows_all + p + 1, t * cols_all + q + 1
            is_kept = kept[i, j] == 1
            is_near = near[i, j] == 1

            def place(l):
                return pl.ds(r * half + t * chunks + l, width, stride=tiles * chunks)

            @pl.when(jnp.logical_and(is_kept, is_near))
            def _():
                exact = dot_half(frow_h[r], scol_h[t]) + (
                    dot_half(frow_h[r], scol_l[t]) + dot_half(frow_l[r], scol_h[t])
                )
                for l in range(chunks):
                    result[place(l), :] = (
                        current[place(l), :] - exact[:, l * BLOCK : (l + 1) * BLOCK]
                    )

            @pl.when(jnp.logical_and(is_kept, jnp.logical_not(is_near)))
            def _():
                rough = dot_half(frow_h[r], scol_h[t]) / scale[i, j]
                for l in range(chunks):
                    far = current[place(l), :] - rough[:, l * BLOCK : (l + 1) * BLOCK]
                    result[place(l), :] = far.astype(jnp.bfloat16).astype(jnp.float32)

            @pl.when(jnp.logical_not(is_kept))
            def _():
                for l in range(chunks):
                    result[place(l), :] = jnp.zeros((width, BLOCK), jnp.float32)

        store = pltpu.make_async_copy(
            result.at[pl.ds(r * half, half)], out_hbm.at[pl.ds(r * half, half)], sems.at[tiles + r]
        )
        store.start()
        stores.append(store)
    for store in stores:
        store.wait()


def update(kept, near, scale, upper, inverse, rows, cols, trailing):
    tiles, pieces, side, width = cols.shape
    vmem = pl.BlockSpec(memory_space=pltpu.VMEM)
    smem = pl.BlockSpec(memory_space=pltpu.SMEM)
    hbm = pl.BlockSpec(memory_space=pltpu.HBM)
    flat = trailing.reshape(trailing.size // BLOCK, BLOCK)
    shape = jax.ShapeDtypeStruct
    return pl.pallas_call(
        update_kernel,
        out_shape=(
            shape(flat.shape, jnp.float32),
            shape((tiles, side, width), jnp.float32),
            shape((side, side), jnp.float32),
        ),
        in_specs=[smem, smem, smem, vmem, vmem, vmem, vmem, hbm],
        out_specs=(hbm, vmem, vmem),
        scratch_shapes=[
            pltpu.VMEM(flat.shape, jnp.float32),
            pltpu.VMEM(flat.shape, jnp.float32),
            pltpu.VMEM((tiles, width, width), jnp.float32),
            pltpu.VMEM((tiles, width, width), jnp.bfloat16),
            pltpu.VMEM((tiles, width, width), jnp.bfloat16),
            pltpu.VMEM((tiles, width, width), jnp.bfloat16),
            pltpu.VMEM((tiles, width, width), jnp.bfloat16),
            pltpu.VMEM((width, side), jnp.float32),
            pltpu.SemaphoreType.DMA((2 * tiles,)),
        ],
        compiler_params=pltpu.CompilerParams(vmem_limit_bytes=45 << 20),
        name="update",
    )(kept, near, scale, upper, inverse, rows, cols, flat)


def panel_kernel(
    pack, own, upper, inverse, rows, cols, gathered, first, turned, trail, extra, work,
    local_sems, turn_sems, send1, recv1, send2, recv2, send3, recv3, send4, recv4,
):
    p, q = lax.axis_index("prow"), lax.axis_index("pcol")
    n, m = lax.axis_size("prow"), lax.axis_size("pcol")
    keep, across = gathered.shape[1], rows.shape[2]
    mesh_id = pl.DeviceIdType.MESH

    def others(me, count, body):
        def step(s, carry):
            body(lax.rem(me + s, count))
            return carry

        lax.fori_loop(1, count, step, 0)

    barrier = pltpu.get_barrier_semaphore()

    def greet(a, b):
        pl.semaphore_signal(barrier, inc=1, device_id=(a, b), device_id_type=mesh_id)

    others(p, n, lambda a: greet(a, q))
    others(q, m, lambda b: greet(p, b))

    @pl.when(p != q)
    def _():
        greet(q, p)

    pl.semaphore_wait(barrier, n + m - 2 + (p != q).astype(jnp.int32))

    def remote(src, dst, send, recv, a, b):
        return pltpu.make_async_remote_copy(
            src_ref=src, dst_ref=dst, send_sem=send, recv_sem=recv,
            device_id=(a, b), device_id_type=mesh_id,
        )

    slot = lax.rem(p + m - q, m)
    mine = pltpu.make_async_copy(pack, first.at[slot], local_sems.at[0])
    mine.start()

    def first_copy(a, sender):
        at = lax.rem(sender + m - q, m)
        return remote(pack, first.at[at], send1.at[a], recv1.at[sender], a, q)

    others(p, n, lambda a: first_copy(a, p).start())

    swap = remote(own, turned, turn_sems.at[0], turn_sems.at[1], q, p)
    stay = pltpu.make_async_copy(own, turned, local_sems.at[1])

    @pl.when(p != q)
    def _():
        swap.start()

    @pl.when(p == q)
    def _():
        stay.start()

    mine.wait()
    others(p, n, lambda a: first_copy(a, a).wait_recv())

    part = first.at[pl.ds(0, keep)]
    block = pltpu.make_async_copy(part, gathered.at[q], local_sems.at[2])
    block.start()

    def second_copy(b, sender):
        return remote(part, gathered.at[sender], send2.at[b], recv2.at[sender], p, b)

    others(q, m, lambda b: second_copy(b, q).start())

    @pl.when(p != q)
    def _():
        swap.wait()

    @pl.when(p == q)
    def _():
        stay.wait()

    core = lax.rem(p, 2)
    other = p + 1 - 2 * core
    held = pltpu.make_async_copy(turned.at[core], cols.at[core, p], local_sems.at[3])
    held.start()

    def fourth_copy(a, sender, tile):
        return remote(
            turned.at[tile], cols.at[tile, sender], send4.at[a], recv4.at[sender], a, q
        )

    others(p, n, lambda a: fourth_copy(a, p, lax.rem(a, 2)).start())

    block.wait()
    others(q, m, lambda b: second_copy(b, b).wait_recv())

    y, x = q // across, lax.rem(q, across)
    whole = [
        pltpu.make_async_copy(own.at[t], rows.at[t, y, x], local_sems.at[4 + t])
        for t in range(2)
    ]
    for copy in whole:
        copy.start()

    def near_x(to, sender):
        return remote(
            own.at[0], rows.at[0, y, sender], send3.at[0, to], recv3.at[0, sender],
            p, y * across + to,
        )

    def near_y(to, sender):
        return remote(
            own.at[1], rows.at[1, sender, x], send3.at[1, to], recv3.at[1, sender],
            p, to * across + x,
        )

    def far_y(to, sender):
        part = rows.at[0, sender]
        return remote(part, part, send3.at[2, to], recv3.at[2, sender], p, to * across + x)

    def far_x(to, sender):
        part = rows.at[1, :, sender]
        return remote(part, part, send3.at[3, to], recv3.at[3, sender], p, y * across + to)

    others(x, across, lambda b: near_x(b, x).start())
    others(y, across, lambda b: near_y(b, y).start())

    def between():
        for copy in whole:
            copy.wait()
        others(x, across, lambda b: near_x(b, b).wait_recv())
        others(y, across, lambda b: near_y(b, b).wait_recv())
        others(y, across, lambda b: far_y(b, y).start())
        others(x, across, lambda b: far_x(b, x).start())

    cholesky_kernel(gathered, upper, inverse, trail, extra, work, between)

    held.wait()
    others(p, n, lambda a: fourth_copy(a, a, core).wait_recv())
    partner = remote(cols.at[core], cols.at[core], turn_sems.at[2], turn_sems.at[3], other, q)
    partner.start()
    others(y, across, lambda b: far_y(b, b).wait_recv())
    others(x, across, lambda b: far_x(b, b).wait_recv())
    partner.wait()
    others(p, n, lambda a: first_copy(a, p).wait_send())
    others(q, m, lambda b: second_copy(b, q).wait_send())
    others(x, across, lambda b: near_x(b, x).wait_send())
    others(y, across, lambda b: near_y(b, y).wait_send())
    others(y, across, lambda b: far_y(b, y).wait_send())
    others(x, across, lambda b: far_x(b, x).wait_send())
    others(p, n, lambda a: fourth_copy(a, p, lax.rem(a, 2)).wait_send())


def panel_step(pack, own):
    n, m = lax.axis_size("prow"), lax.axis_size("pcol")
    tiles, side, width = own.shape
    vmem = pl.BlockSpec(memory_space=pltpu.VMEM)
    shape = jax.ShapeDtypeStruct
    dma = pltpu.SemaphoreType.DMA
    return pl.pallas_call(
        panel_kernel,
        out_shape=(
            shape((width, width), jnp.float32),
            shape((width, width), jnp.float32),
            shape((tiles, m // ACROSS, ACROSS, side, width), jnp.float32),
            shape((tiles, n, side, width), jnp.float32),
        ),
        in_specs=[vmem, vmem],
        out_specs=(vmem, vmem, vmem, vmem),
        scratch_shapes=[
            pltpu.VMEM((m, n // 2 + 1, SUB, BLOCK), jnp.float32),
            pltpu.VMEM((n, SUB, BLOCK), jnp.float32),
            pltpu.VMEM((tiles, side, width), jnp.float32),
            pltpu.VMEM((width, width), jnp.float32),
            pltpu.VMEM((width, width), jnp.float32),
            pltpu.VMEM((BLOCK, 2 * BLOCK), jnp.float32),
            dma((6,)), dma((4,)),
            dma((n,)), dma((n,)), dma((m,)), dma((m,)),
            dma((4, ACROSS)), dma((4, ACROSS)), dma((n,)), dma((n,)),
        ],
        compiler_params=pltpu.CompilerParams(
            collective_id=0, has_side_effects=True, vmem_limit_bytes=32 << 20
        ),
        cost_estimate=pl.CostEstimate(
            flops=1 << 34, bytes_accessed=1 << 26, transcendentals=0
        ),
        name="panel",
    )(pack, own)


def per_device(diag_tile, panel, trailing, kept, precision, tile_scale):
    side = diag_tile.shape[0]
    own = jnp.transpose(panel[:, 0], (0, 2, 1))
    pack = diag_tile.T.reshape(side // SUB, SUB, side).transpose(1, 0, 2).reshape(SUB, BLOCK)
    upper, inverse, rows, cols = panel_step(pack, own)
    updated, factor, diag_out = update(
        kept, precision, tile_scale, upper, inverse, rows, cols, trailing
    )
    factor_out = jnp.transpose(factor, (0, 2, 1))[:, None]
    return (diag_out, factor_out, updated.reshape(trailing.shape))


def solution(mesh):
    in_specs = (
        P("prow", "pcol"),
        P(None, "prow", None, "pcol"),
        P(None, "prow", None, None, "pcol", None),
        P(),
        P(),
        P(),
    )
    out_specs = (
        P("prow", "pcol"),
        P(None, "prow", None, "pcol"),
        P(None, "prow", None, None, "pcol", None),
    )
    return jax.shard_map(
        per_device, mesh=mesh, in_specs=in_specs, out_specs=out_specs, check_vma=False
    )
```

```python
import jax
import jax.numpy as jnp
from jax import lax
from jax.experimental import pallas as pl
from jax.experimental.pallas import tpu as pltpu
from jax.sharding import PartitionSpec as P

BLOCK = 128
PANEL = 16
SUB = 8
ACROSS = 4
FULL = lax.Precision.HIGHEST


def dot_f32(a, b, ca, cb):
    return lax.dot_general(
        a, b, (((ca,), (cb,)), ((), ())), precision=FULL, preferred_element_type=jnp.float32
    )


def factor_block(work):
    sub = lax.broadcasted_iota(jnp.int32, (SUB, BLOCK), 0)
    halves = PANEL // SUB
    for base in range(0, BLOCK, PANEL):
        rows = [work[base + SUB * h : base + SUB * (h + 1), :] for h in range(halves)]
        left = [r[:, :BLOCK] for r in rows]
        right = [r[:, BLOCK:] for r in rows]
        cols = {}
        for k in range(PANEL):
            for h in range(k // SUB, halves):
                cols[k, h] = jnp.broadcast_to(
                    left[h][:, base + k : base + k + 1], (SUB, BLOCK)
                )
        scale = [jnp.ones((SUB, BLOCK), jnp.float32) for _ in range(halves)]
        for m in range(PANEL):
            own, at = m // SUB, m % SUB
            pivot = jnp.broadcast_to(cols[m, own][at : at + 1, :], (SUB, BLOCK))
            root = lax.rsqrt(pivot)
            scale[own] = jnp.where(sub == at, root, scale[own])
            lower = {h: cols[m, h] * root for h in range(own, halves)}
            for k in range(m + 1, PANEL):
                factor = jnp.broadcast_to(
                    lower[k // SUB][k % SUB : k % SUB + 1, :], (SUB, BLOCK)
                )
                for h in range(k // SUB, halves):
                    cols[k, h] = cols[k, h] - lower[h] * factor
            source_left = jnp.broadcast_to(left[own][at : at + 1, :], (SUB, BLOCK)) * root
            source_right = jnp.broadcast_to(right[own][at : at + 1, :], (SUB, BLOCK)) * root
            for h in range(own, halves):
                weight = jnp.where(sub > at, lower[h], 0.0) if h == own else lower[h]
                left[h] = left[h] - weight * source_left
                right[h] = right[h] - weight * source_right
        left = [x * s for x, s in zip(left, scale)]
        right = [x * s for x, s in zip(right, scale)]
        upper = jnp.concatenate(left, 0)
        both = jnp.concatenate([upper, jnp.concatenate(right, 0)], 1)
        work[base : base + PANEL, :] = both
        rest = base + PANEL
        if rest < BLOCK:
            change = dot_f32(upper.T[rest:, :], both, 1, 0)
            work[rest:, :] = work[rest:, :] - change


def cholesky_kernel(gathered, u_ref, v_ref, trail, extra, work, between):
    width = u_ref.shape[0]
    assemble(gathered, trail, extra)
    u_ref[...] = jnp.zeros_like(u_ref)
    v_ref[...] = jnp.zeros_like(v_ref)
    extra[...] = jnp.zeros_like(extra)
    row = lax.broadcasted_iota(jnp.int32, (BLOCK, BLOCK), 0)
    col = lax.broadcasted_iota(jnp.int32, (BLOCK, BLOCK), 1)
    eye = (row == col).astype(jnp.float32)
    for base in range(0, width, BLOCK):
        here = slice(base, base + BLOCK)
        end = base + BLOCK
        work[:, :BLOCK] = trail[here, here]
        work[:, BLOCK:] = eye
        factor_block(work)
        if base == 0:
            between()
        inverse = work[:, BLOCK:]
        u_ref[here, here] = jnp.where(row <= col, work[:, :BLOCK], 0.0)
        v_ref[here, here] = inverse
        if base:
            v_ref[here, :base] = dot_f32(inverse, extra[here, :base], 1, 0)
        if end < width:
            upper = dot_f32(inverse, trail[here, end:], 1, 0)
            u_ref[here, end:] = upper
            turned = upper.T
            for low in range(end, width, BLOCK):
                piece = turned[low - end : low - end + BLOCK, :]
                trail[low : low + BLOCK, low:] = trail[low : low + BLOCK, low:] - dot_f32(
                    piece, upper[:, low - end :], 1, 0
                )
            extra[end:, :end] = extra[end:, :end] - dot_f32(turned, v_ref[here, :end], 1, 0)


def split(x):
    high = x.astype(jnp.bfloat16)
    return high, (x - high.astype(jnp.float32)).astype(jnp.bfloat16)


def assemble(gathered, a_ref, direct):
    count, width = gathered.shape[0], a_ref.shape[0]
    side = width // count
    per = BLOCK // side
    lane = lax.broadcasted_iota(jnp.int32, (SUB, BLOCK), 1) // side
    for q in range(count):
        held = {}
        for o in range(count // 2 + 1):
            if o < count // 2 or q < count // 2:
                held[(q + o) % count] = gathered[q, o]
        for g in range(side // SUB):
            for tile in range(count // per):
                total = jnp.zeros((SUB, BLOCK), jnp.float32)
                for e in range(per):
                    piece = held.get(tile * per + e)
                    if piece is not None:
                        shift = (e - g) % per * side
                        moved = pltpu.roll(piece, shift, 1) if shift else piece
                        total = jnp.where(lane == e, moved, total)
                low = q * side + g * SUB
                direct[low : low + SUB, tile * BLOCK : (tile + 1) * BLOCK] = total
    row = lax.broadcasted_iota(jnp.int32, (BLOCK, BLOCK), 0) // side
    col = lax.broadcasted_iota(jnp.int32, (BLOCK, BLOCK), 1) // side
    for i in range(0, width, BLOCK):
        for j in range(i, width, BLOCK):
            here = direct[i : i + BLOCK, j : j + BLOCK]
            there = direct[j : j + BLOCK, i : i + BLOCK].T
            if i == j:
                there = jnp.where(row == col, 0.0, there)
            a_ref[i : i + BLOCK, j : j + BLOCK] = here + there


def update_kernel(
    kept, near, scale, u_ref, rows_ref, cols_ref, trailing, out_hbm, factor_ref, diag_ref,
    current, result, frow_h, frow_l, scol_h, scol_l, turned, sems,
):
    tiles, side, width = factor_ref.shape
    p, q = lax.axis_index("prow"), lax.axis_index("pcol")
    rows_all = lax.axis_size("prow")
    cols_all = lax.axis_size("pcol")
    half = current.shape[0] // tiles
    chunks = width // BLOCK
    loads = [
        pltpu.make_async_copy(
            trailing.at[pl.ds(r * half, half)], current.at[pl.ds(r * half, half)], sems.at[r]
        )
        for r in range(tiles)
    ]
    for load in loads:
        load.start()
    turned[...] = u_ref[pl.ds(pl.multiple_of(q * side, side), side), :].T
    diag_ref[...] = turned[pl.ds(pl.multiple_of(p * side, side), side), :]
    for r in range(tiles):
        keep = kept[r * rows_all + p + 1, 0].astype(jnp.float32)
        solved = rows_ref[r] * keep
        factor_ref[r] = rows_ref[r, pl.ds(pl.multiple_of(q * side, side), side), :] * keep
        high, low = split(solved.T)
        frow_h[r] = high
        frow_l[r] = low
    for t in range(tiles):
        keep = kept[t * cols_all + q + 1, 0].astype(jnp.float32)
        high, low = split(cols_ref[t] * keep)
        scol_h[t] = high
        scol_l[t] = low

    def dot_half(a, b):
        return jnp.dot(a, b, preferred_element_type=jnp.float32)

    stores = []
    for r in range(tiles):
        loads[r].wait()
        for t in range(tiles):
            i, j = r * rows_all + p + 1, t * cols_all + q + 1
            is_kept = kept[i, j] == 1
            is_near = near[i, j] == 1

            def place(l):
                return pl.ds(r * half + t * chunks + l, width, stride=tiles * chunks)

            @pl.when(jnp.logical_and(is_kept, is_near))
            def _():
                exact = dot_half(frow_h[r], scol_h[t]) + (
                    dot_half(frow_h[r], scol_l[t]) + dot_half(frow_l[r], scol_h[t])
                )
                for l in range(chunks):
                    result[place(l), :] = (
                        current[place(l), :] - exact[:, l * BLOCK : (l + 1) * BLOCK]
                    )

            @pl.when(jnp.logical_and(is_kept, jnp.logical_not(is_near)))
            def _():
                rough = dot_half(frow_h[r], scol_h[t]) / scale[i, j]
                for l in range(chunks):
                    far = current[place(l), :] - rough[:, l * BLOCK : (l + 1) * BLOCK]
                    result[place(l), :] = far.astype(jnp.bfloat16).astype(jnp.float32)

            @pl.when(jnp.logical_not(is_kept))
            def _():
                for l in range(chunks):
                    result[place(l), :] = jnp.zeros((width, BLOCK), jnp.float32)

        store = pltpu.make_async_copy(
            result.at[pl.ds(r * half, half)], out_hbm.at[pl.ds(r * half, half)], sems.at[tiles + r]
        )
        store.start()
        stores.append(store)
    for store in stores:
        store.wait()


def update(kept, near, scale, upper, rows, cols, side, trailing):
    tiles, width = cols.shape[:2]
    vmem = pl.BlockSpec(memory_space=pltpu.VMEM)
    smem = pl.BlockSpec(memory_space=pltpu.SMEM)
    hbm = pl.BlockSpec(memory_space=pltpu.HBM)
    flat = trailing.reshape(trailing.size // BLOCK, BLOCK)
    shape = jax.ShapeDtypeStruct
    return pl.pallas_call(
        update_kernel,
        out_shape=(
            shape(flat.shape, jnp.float32),
            shape((tiles, side, width), jnp.float32),
            shape((side, side), jnp.float32),
        ),
        in_specs=[smem, smem, smem, vmem, vmem, vmem, hbm],
        out_specs=(hbm, vmem, vmem),
        scratch_shapes=[
            pltpu.VMEM(flat.shape, jnp.float32),
            pltpu.VMEM(flat.shape, jnp.float32),
            pltpu.VMEM((tiles, width, width), jnp.bfloat16),
            pltpu.VMEM((tiles, width, width), jnp.bfloat16),
            pltpu.VMEM((tiles, width, width), jnp.bfloat16),
            pltpu.VMEM((tiles, width, width), jnp.bfloat16),
            pltpu.VMEM((width, side), jnp.float32),
            pltpu.SemaphoreType.DMA((2 * tiles,)),
        ],
        compiler_params=pltpu.CompilerParams(vmem_limit_bytes=45 << 20),
        name="update",
    )(kept, near, scale, upper, rows, cols, flat)


def panel_kernel(
    pack, own, upper, row_solved, col_solved,
    inverse, rows, cols, gathered, first, turned, trail, extra, work,
    local_sems, turn_sems, send1, recv1, send2, recv2, send3, recv3, send4, recv4,
):
    p, q = lax.axis_index("prow"), lax.axis_index("pcol")
    n, m = lax.axis_size("prow"), lax.axis_size("pcol")
    keep, across, width = gathered.shape[1], rows.shape[2], upper.shape[0]
    mesh_id = pl.DeviceIdType.MESH

    def others(me, count, body):
        def step(s, carry):
            body(lax.rem(me + s, count))
            return carry

        lax.fori_loop(1, count, step, 0)

    barrier = pltpu.get_barrier_semaphore()

    def greet(a, b):
        pl.semaphore_signal(barrier, inc=1, device_id=(a, b), device_id_type=mesh_id)

    others(p, n, lambda a: greet(a, q))
    others(q, m, lambda b: greet(p, b))

    @pl.when(p != q)
    def _():
        greet(q, p)

    pl.semaphore_wait(barrier, n + m - 2 + (p != q).astype(jnp.int32))

    def remote(src, dst, send, recv, a, b):
        return pltpu.make_async_remote_copy(
            src_ref=src, dst_ref=dst, send_sem=send, recv_sem=recv,
            device_id=(a, b), device_id_type=mesh_id,
        )

    core = lax.rem(p, 2)
    other = p + 1 - 2 * core

    slot = lax.rem(p + m - q, m)
    mine = pltpu.make_async_copy(pack, first.at[slot], local_sems.at[0])
    mine.start()

    def first_copy(a, sender):
        at = lax.rem(sender + m - q, m)
        return remote(pack, first.at[at], send1.at[a], recv1.at[sender], a, q)

    others(p, n, lambda a: first_copy(a, p).start())

    swap = remote(own, turned, turn_sems.at[0], turn_sems.at[1], q, p)
    stay = pltpu.make_async_copy(own, turned, local_sems.at[1])

    @pl.when(p != q)
    def _():
        swap.start()

    @pl.when(p == q)
    def _():
        stay.start()

    mine.wait()
    others(p, n, lambda a: first_copy(a, a).wait_recv())

    share = pl.ds(core * (keep // 2), keep // 2)
    part = first.at[share]
    block = pltpu.make_async_copy(part, gathered.at[q, share], local_sems.at[2])
    block.start()

    def second_copy(b, sender):
        return remote(part, gathered.at[sender, share], send2.at[b], recv2.at[sender], p, b)

    others(q, m, lambda b: second_copy(b, q).start())

    block.wait()
    others(q, m, lambda b: second_copy(b, b).wait_recv())
    fill = remote(
        gathered.at[:, share], gathered.at[:, share], turn_sems.at[4], turn_sems.at[5], other, q
    )
    fill.start()

    y, x = q // across, lax.rem(q, across)
    whole = [
        pltpu.make_async_copy(own.at[t], rows.at[t, y, x], local_sems.at[4 + t])
        for t in range(2)
    ]
    for copy in whole:
        copy.start()

    def near_x(to, sender):
        return remote(
            own.at[0], rows.at[0, y, sender], send3.at[0, to], recv3.at[0, sender],
            p, y * across + to,
        )

    def near_y(to, sender):
        return remote(
            own.at[1], rows.at[1, sender, x], send3.at[1, to], recv3.at[1, sender],
            p, to * across + x,
        )

    def far_y(to, sender):
        part = rows.at[0, sender]
        return remote(part, part, send3.at[2, to], recv3.at[2, sender], p, to * across + x)

    def far_x(to, sender):
        part = rows.at[1, :, sender]
        return remote(part, part, send3.at[3, to], recv3.at[3, sender], p, y * across + to)

    others(x, across, lambda b: near_x(b, x).start())
    others(y, across, lambda b: near_y(b, y).start())

    @pl.when(p != q)
    def _():
        swap.wait()

    @pl.when(p == q)
    def _():
        stay.wait()

    held = pltpu.make_async_copy(turned.at[core], cols.at[core, p], local_sems.at[3])
    held.start()

    def fourth_copy(a, sender, tile):
        return remote(
            turned.at[tile], cols.at[tile, sender], send4.at[a], recv4.at[sender], a, q
        )

    others(p, n, lambda a: fourth_copy(a, p, lax.rem(a, 2)).start())

    def between():
        for copy in whole:
            copy.wait()
        others(x, across, lambda b: near_x(b, b).wait_recv())
        others(y, across, lambda b: near_y(b, b).wait_recv())
        others(y, across, lambda b: far_y(b, y).start())
        others(x, across, lambda b: far_x(b, x).start())

    fill.wait()
    cholesky_kernel(gathered, upper, inverse, trail, extra, work, between)

    def solve(piece):
        mid = width // 2
        top = dot_f32(inverse[:mid, :mid], piece[:mid, :], 1, 0)
        low = dot_f32(inverse[mid:, :], piece, 1, 0)
        return jnp.concatenate([top, low], 0)

    others(y, across, lambda b: far_y(b, b).wait_recv())
    others(x, across, lambda b: far_x(b, b).wait_recv())
    row_solved[0] = solve(rows[0].reshape(width, width))
    held.wait()
    others(p, n, lambda a: fourth_copy(a, a, core).wait_recv())
    partner = remote(cols.at[core], cols.at[core], turn_sems.at[2], turn_sems.at[3], other, q)
    partner.start()
    row_solved[1] = solve(rows[1].reshape(width, width))
    col_solved[core] = solve(cols[core].reshape(width, width))
    partner.wait()
    col_solved[1 - core] = solve(cols[1 - core].reshape(width, width))
    others(p, n, lambda a: first_copy(a, p).wait_send())
    others(q, m, lambda b: second_copy(b, q).wait_send())
    others(x, across, lambda b: near_x(b, x).wait_send())
    others(y, across, lambda b: near_y(b, y).wait_send())
    others(y, across, lambda b: far_y(b, y).wait_send())
    others(x, across, lambda b: far_x(b, x).wait_send())
    others(p, n, lambda a: fourth_copy(a, p, lax.rem(a, 2)).wait_send())


def panel_step(pack, own):
    n, m = lax.axis_size("prow"), lax.axis_size("pcol")
    tiles, side, width = own.shape
    vmem = pl.BlockSpec(memory_space=pltpu.VMEM)
    shape = jax.ShapeDtypeStruct
    dma = pltpu.SemaphoreType.DMA
    return pl.pallas_call(
        panel_kernel,
        out_shape=(
            shape((width, width), jnp.float32),
            shape((tiles, width, width), jnp.float32),
            shape((tiles, width, width), jnp.float32),
        ),
        in_specs=[vmem, vmem],
        out_specs=(vmem, vmem, vmem),
        scratch_shapes=[
            pltpu.VMEM((width, width), jnp.float32),
            pltpu.VMEM((tiles, m // ACROSS, ACROSS, side, width), jnp.float32),
            pltpu.VMEM((tiles, n, side, width), jnp.float32),
            pltpu.VMEM((m, n // 2 + 2, SUB, BLOCK), jnp.float32),
            pltpu.VMEM((n, SUB, BLOCK), jnp.float32),
            pltpu.VMEM((tiles, side, width), jnp.float32),
            pltpu.VMEM((width, width), jnp.float32),
            pltpu.VMEM((width, width), jnp.float32),
            pltpu.VMEM((BLOCK, 2 * BLOCK), jnp.float32),
            dma((6,)), dma((6,)),
            dma((n,)), dma((n,)), dma((m,)), dma((m,)),
            dma((4, ACROSS)), dma((4, ACROSS)), dma((n,)), dma((n,)),
        ],
        compiler_params=pltpu.CompilerParams(
            collective_id=0, has_side_effects=True, vmem_limit_bytes=32 << 20
        ),
        cost_estimate=pl.CostEstimate(
            flops=1 << 34, bytes_accessed=1 << 26, transcendentals=0
        ),
        name="panel",
    )(pack, own)


def per_device(diag_tile, panel, trailing, kept, precision, tile_scale):
    side = diag_tile.shape[0]
    own = jnp.transpose(panel[:, 0], (0, 2, 1))
    pack = diag_tile.T.reshape(side // SUB, SUB, side).transpose(1, 0, 2).reshape(SUB, BLOCK)
    upper, rows, cols = panel_step(pack, own)
    updated, factor, diag_out = update(
        kept, precision, tile_scale, upper, rows, cols, side, trailing
    )
    factor_out = jnp.transpose(factor, (0, 2, 1))[:, None]
    return (diag_out, factor_out, updated.reshape(trailing.shape))


def solution(mesh):
    in_specs = (
        P("prow", "pcol"),
        P(None, "prow", None, "pcol"),
        P(None, "prow", None, None, "pcol", None),
        P(),
        P(),
        P(),
    )
    out_specs = (
        P("prow", "pcol"),
        P(None, "prow", None, "pcol"),
        P(None, "prow", None, None, "pcol", None),
    )
    return jax.shard_map(
        per_device, mesh=mesh, in_specs=in_specs, out_specs=out_specs, check_vma=False
    )
```
